256 devices in a mesh: row: 16 (over y_hi, z), col: 16 (over x, y_lo, core).
Axes of the slice: x: 4, y: 4 (y_hi: 2, y_lo: 2; y = y_hi * 2 + y_lo), z: 8, core: 2. Of those that a mesh axis runs over, the one named last changes fastest.
Arguments:
- amplitudes: bfloat16 [49152, 12288], P('row', 'col'), may hold values from -6 to 6
- pair_mask: int32 [192, 48], P('row', 'col'), may hold values 0 or 1
- integrals: bfloat16 [16, 16, 2, 256, 256], P('row', 'col'), may hold values from -0.25 to 0.25
- tile_list: int32 [16, 16, 2], P('row', 'col'), may hold values from 0 to 2, as said below
- tile_count: int32 [16, 16], P('row', 'col'), may hold values from 1 to 2, as said below
- owner: int32 [4, 16], P(None, 'col'), may hold values from 0 to 15, as said below
Outputs:
- ladder: bfloat16 [49152, 4096], P('row', 'col')
The draws below stay inside these ranges and needn't reach their ends.
Inputs may be any that keep to these rules, and one draw needn't show every extreme that they name: `owner`: within a column the 4 owners differ. `tile_count`: some panel that serves a step has all 2 slots live. `tile_list`: the live slots of a panel name distinct cd tile pairs; entries past the count are in range and unused.
All inputs are finite; a program needn't handle non-finite values. No bound on the sum of `pair_mask` on one device may be relied on, other than what follows from the above.
Results may differ from the reference program's by a relative error of at most 0.001.
Values may be sent and summed in bfloat16 or wider, within the bound.
A program may use at most 128 MiB of HBM per device.

```python
import jax
import jax.numpy as jnp
from jax import lax

BLK = 256
NCD = 3
CAP = 2
STEPS = 4
TP = 256
PAIRS = 49152
NBLK = 192
CDT = 48
N_ROW = 16
N_COL = 16


def owner_table(key):
    base_key = jax.random.fold_in(key, 11)
    column_keys = jax.random.split(base_key, N_COL)
    orders = jax.vmap(lambda single: jax.random.permutation(single, N_ROW))(column_keys)
    leading = orders[0]
    top_place = jnp.argmax(leading == N_ROW - 1)
    swapped = leading.at[top_place].set(leading[0]).at[0].set(N_ROW - 1)
    orders = orders.at[0].set(swapped)
    return jnp.transpose(orders[:, :STEPS]).astype(jnp.int32)


def draw_owner(key, part):
    return owner_table(key)


def draw_tile_count(key, part):
    plan = owner_table(key)
    flips = jax.random.randint(jax.random.fold_in(key, 23), (N_ROW, N_COL), 0, 3)
    counts = jnp.where(flips == 0, CAP, 1).astype(jnp.int32)
    counts = counts.at[plan[0, 0], 0].set(CAP)
    counts = counts.at[plan[1, 0], 0].set(1)
    return counts


def draw_tile_list(key, part):
    panel_keys = jax.random.split(jax.random.fold_in(key, 37), N_ROW * N_COL)
    orders = jax.vmap(lambda single: jax.random.permutation(single, NCD))(panel_keys)
    return orders[:, :CAP].reshape(N_ROW, N_COL, CAP).astype(jnp.int32)


def touch_ends(array, own_key, smallest, top_value):
    extent = array.shape
    spot = [jax.random.randint(jax.random.fold_in(own_key, axis), (), 0, extent[axis]) for axis in range(len(extent))]
    array = array.at[tuple(spot)].set(smallest)
    longest = extent.index(max(extent))
    spot[longest] = (spot[longest] + 1) % extent[longest]
    return array.at[tuple(spot)].set(top_value)


def levels(stream_key, extent, cuts, low, high):
    loudness, own = 1.0, jax.random.fold_in(stream_key, 6)
    for position, shards_of in cuts:
        heights = jnp.exp(jax.random.uniform(jax.random.fold_in(own, position), (shards_of,), jnp.float32, low / len(cuts), high / len(cuts)))
        loudness = loudness * jnp.repeat(heights, extent[position] // shards_of).reshape([-1 if axis == position else 1 for axis in range(len(extent))])
    return loudness


def scatter_about(stream_key, dims, deviation, reach, shards=(), kind=jnp.bfloat16):
    level = levels(stream_key, dims, shards, -0.22, 0.18) if shards else 1.0
    values = jax.random.normal(stream_key, dims, jnp.float32) * deviation * level
    return jnp.minimum(jnp.maximum(values, -reach), reach).astype(kind)


def setup_inputs(seed: int = 0) -> dict:
    key_list = jax.random.split(jax.random.key(seed), 7)
    amplitudes = scatter_about(key_list[0], (PAIRS, CDT * TP), 1.0, 6.0, ((0, 16), (1, 16)))
    pair_mask = touch_ends((jax.random.randint(key_list[1], (NBLK, CDT), 0, 4) < 3).astype(jnp.int32), jax.random.fold_in(key_list[1], 1), 0, 1)
    integrals = scatter_about(key_list[2], (N_ROW, N_COL, CAP, TP, TP), (2 * TP) ** -0.5, 0.25, ((0, 16), (1, 16)))
    tile_list = draw_tile_list(jax.random.fold_in(key_list[6], 71), 0)
    tile_count = draw_tile_count(jax.random.fold_in(key_list[6], 71), 0)
    owner = draw_owner(jax.random.fold_in(key_list[6], 71), 0)
    return dict(amplitudes=amplitudes, pair_mask=pair_mask, integrals=integrals, tile_list=tile_list, tile_count=tile_count, owner=owner)


def reference(amplitudes, pair_mask, integrals, tile_list, tile_count, owner):
    pair_rows = amplitudes.shape[0]
    block_mask = jnp.repeat(pair_mask, BLK, axis=0).astype(amplitudes.dtype)

    def column(column_id):
        running = jnp.zeros((pair_rows, TP), jnp.float32)
        for grid_step in range(STEPS):
            source_group = ((column_id - grid_step) % N_COL).astype(jnp.int32)
            holder = owner[grid_step, column_id].astype(jnp.int32)
            for slot_index in range(CAP):
                tile_index = (source_group * NCD + tile_list[holder, column_id, slot_index]).astype(jnp.int32)
                tile_block = lax.dynamic_slice_in_dim(amplitudes, tile_index * TP, TP, 1)
                block_scale = lax.dynamic_slice_in_dim(block_mask, tile_index, 1, 1)
                product = jnp.dot(tile_block * block_scale, integrals[holder, column_id, slot_index], preferred_element_type=jnp.float32)
                running = running + jnp.where(slot_index < tile_count[holder, column_id], product, jnp.zeros_like(product))
        return running.astype(jnp.bfloat16)

    stacked = lax.map(column, jnp.arange(N_COL, dtype=jnp.int32))
    return jnp.transpose(stacked, (1, 0, 2)).reshape(pair_rows, N_COL * TP)
```

```python
import functools

import jax
import jax.numpy as jnp
from jax import lax
from jax.experimental import pallas as pl
from jax.experimental.pallas import tpu as pltpu
from jax.sharding import PartitionSpec as P

MESH = pl.DeviceIdType.MESH
F32 = jnp.float32
BF16 = jnp.bfloat16
LINK = jnp.int16
TOP = 32767.0
TINY = 1e-33


def kernel(
    rows_of, cols_of, owner_ref, list_ref, count_ref, mask_ref, amp, panel, out,
    both, maskv, meta, meta_in, piece_in, fac_out, fac_a, fac_b, q_out, p_a, p_b,
    w_a, w_b, local, t_own, s_out, s_scale, r_one, r_one_scale, t_out, t_scale, r_two, r_two_scale, result,
    amp_sem, amp_send, amp_recv, a2a_send, a2a_recv, shift_send, shift_recv,
    ring_send_a, ring_recv_a, ring_send_b, ring_recv_b, one_send, one_recv, two_send, two_recv, out_sem,
):
    r, c = lax.axis_index("row"), lax.axis_index("col")
    depth_z = rows_of // 2
    chips = cols_of // 2
    y, z = r // depth_z, r % depth_z
    chip, core = c // 2, c % 2
    y_lo = chip % 2
    tile = panel.shape[-1]
    strip = tile // rows_of
    blocks, tiles = mask_ref.shape
    block = amp.shape[0] // blocks
    width = amp.shape[1]

    def at_chip(step, same_core=True):
        return lax.rem(chip + step + chips, chips) * 2 + core

    row_id = lax.broadcasted_iota(jnp.int32, (8, 128), 0)
    flags = jnp.zeros((8, 128), F32)
    for k in range(2):
        live = jnp.where(k < count_ref[0, 0], k * tiles + list_ref[0, 0, k], -1)
        flags = flags + jnp.where(row_id == live, 1.0, 0.0)
    meta[...] = flags
    meta_in[r] = flags
    for b in range(blocks):
        for t in range(tiles):
            maskv[core, b : b + 1, t * tile : (t + 1) * tile] = jnp.full(
                (1, tile), mask_ref[b, t].astype(F32), F32
            )

    own_amp = pltpu.make_async_copy(amp, both.at[core], amp_sem.at[0])
    own_amp.start()
    own_piece = pltpu.make_async_copy(
        panel.at[:, pl.ds(pl.multiple_of(r * strip, strip), strip), :], piece_in.at[r], amp_sem.at[1]
    )
    own_piece.start()

    barrier = pltpu.get_barrier_semaphore()

    def greet(d, carry):
        pl.semaphore_signal(barrier, 1, device_id=(lax.rem(r + d, rows_of), c), device_id_type=MESH)
        return carry

    lax.fori_loop(1, rows_of, greet, 0)
    for step in (1, -1, 2, -2):
        pl.semaphore_signal(barrier, 1, device_id=(r, at_chip(step)), device_id_type=MESH)
    partner = chip * 2 + 1 - core
    pl.semaphore_signal(barrier, 1, device_id=(r, partner), device_id_type=MESH)
    pl.semaphore_wait(barrier, rows_of - 1 + 5)

    def piece_copies(d):
        peer = lax.rem(r + d, rows_of)
        return (
            pltpu.make_async_remote_copy(
                src_ref=panel.at[:, pl.ds(pl.multiple_of(peer * strip, strip), strip), :],
                dst_ref=piece_in.at[r],
                send_sem=a2a_send.at[0, d],
                recv_sem=a2a_recv.at[0, d],
                device_id=(peer, c),
                device_id_type=MESH,
            ),
            pltpu.make_async_remote_copy(
                src_ref=meta,
                dst_ref=meta_in.at[r],
                send_sem=a2a_send.at[1, d],
                recv_sem=a2a_recv.at[1, d],
                device_id=(peer, c),
                device_id_type=MESH,
            ),
        )

    def send_pieces(d, carry):
        for copy in piece_copies(d):
            copy.start()
        return carry

    lax.fori_loop(1, rows_of, send_pieces, 0)

    swaps = (
        pltpu.make_async_remote_copy(
            src_ref=maskv.at[core], dst_ref=maskv.at[core], send_sem=amp_send.at[0], recv_sem=amp_recv.at[0],
            device_id=(r, partner), device_id_type=MESH,
        ),
        pltpu.make_async_remote_copy(
            src_ref=amp, dst_ref=both.at[core], send_sem=amp_send.at[1], recv_sem=amp_recv.at[1],
            device_id=(r, partner), device_id_type=MESH,
        ),
    )
    for copy in swaps:
        copy.start()

    def wait_pieces(d, carry):
        for copy in piece_copies(d):
            copy.wait_recv()
        return carry

    own_piece.wait()
    lax.fori_loop(1, rows_of, wait_pieces, 0)

    chosen = []
    for even_step, odd_step in ((2, 3), (1, 2), (0, 1), (3, 0)):
        chosen.append(owner_ref[even_step * (1 - core) + odd_step * core, 0])
    for slot in (0, 1):
        q_out[slot] = piece_in[chosen[slot]]
        fac_out[slot] = meta_in[chosen[slot]]
    p_b[r, 0] = piece_in[chosen[2]]
    fac_b[0] = meta_in[chosen[2]]

    @pl.when(core == 0)
    def _():
        q_out[2] = piece_in[chosen[3]]
        fac_out[2] = meta_in[chosen[3]]

    @pl.when(core == 1)
    def _():
        p_b[r, 1] = piece_in[chosen[3]]
        fac_b[1] = meta_in[chosen[3]]

    shift_one = (
        pltpu.make_async_remote_copy(
            src_ref=q_out.at[pl.ds(0, 2)], dst_ref=p_a.at[r], send_sem=shift_send.at[0], recv_sem=shift_recv.at[0],
            device_id=(r, at_chip(-1)), device_id_type=MESH,
        ),
        pltpu.make_async_remote_copy(
            src_ref=fac_out.at[pl.ds(0, 2)], dst_ref=fac_a, send_sem=shift_send.at[1], recv_sem=shift_recv.at[1],
            device_id=(r, at_chip(-1)), device_id_type=MESH,
        ),
    )
    shift_two = (
        pltpu.make_async_remote_copy(
            src_ref=q_out.at[2], dst_ref=p_b.at[r, 1], send_sem=shift_send.at[2], recv_sem=shift_recv.at[2],
            device_id=(r, at_chip(-2)), device_id_type=MESH,
        ),
        pltpu.make_async_remote_copy(
            src_ref=fac_out.at[2], dst_ref=fac_b.at[1], send_sem=shift_send.at[3], recv_sem=shift_recv.at[3],
            device_id=(r, at_chip(-2)), device_id_type=MESH,
        ),
    )
    for copy in shift_one:
        copy.start()

    @pl.when(core == 0)
    def _():
        for copy in shift_two:
            copy.start()

    def ring_copy(buf, send, recv, chain, way, step):
        half = lax.rem(y + chain, 2)
        if way == 0:
            block_z, to_z = lax.rem(z - (step - 1) + depth_z, depth_z), lax.rem(z + 1, depth_z)
        else:
            block_z, to_z = lax.rem(z + (step - 1), depth_z), lax.rem(z - 1 + depth_z, depth_z)
        held = buf.at[half * depth_z + block_z]
        return pltpu.make_async_remote_copy(
            src_ref=held, dst_ref=held, send_sem=send.at[chain, way, step], recv_sem=recv.at[chain, way, step],
            device_id=(y * depth_z + to_z, c), device_id_type=MESH,
        )

    def cross_copy(buf, send, recv):
        return pltpu.make_async_remote_copy(
            src_ref=buf.at[r], dst_ref=buf.at[r], send_sem=send.at[0, 0, 0], recv_sem=recv.at[0, 0, 0],
            device_id=(lax.rem(r + depth_z, rows_of), c), device_id_type=MESH,
        )

    reach = (depth_z // 2, (depth_z - 1) // 2)

    def ring_received(buf, send, recv, chain, way, step):
        half = lax.rem(y + chain, 2)
        block_z = lax.rem(z - step + depth_z, depth_z) if way == 0 else lax.rem(z + step, depth_z)
        held = buf.at[half * depth_z + block_z]
        return pltpu.make_async_remote_copy(
            src_ref=held, dst_ref=held, send_sem=send.at[chain, way, step], recv_sem=recv.at[chain, way, step],
            device_id=(r, partner), device_id_type=MESH,
        )

    def ring_step(buf, send, recv, step):
        for chain in (0, 1):
            if step == 1 and chain == 1:
                cross_copy(buf, send, recv).wait_recv()
            for way in (0, 1):
                if 1 < step <= reach[way] + 1:
                    ring_received(buf, send, recv, chain, way, step - 1).wait_recv()
                if step <= reach[way]:
                    ring_copy(buf, send, recv, chain, way, step).start()

    def ring_drain(buf, send, recv):
        cross_copy(buf, send, recv).wait_send()
        for chain in (0, 1):
            for way in (0, 1):
                for step in range(1, reach[way] + 1):
                    ring_copy(buf, send, recv, chain, way, step).wait_send()

    def assemble(fac, strips, weights):
        for slot in (0, 1):
            factors = []
            for k in range(2):
                for t in range(tiles):
                    f = jnp.broadcast_to(fac[slot, k * tiles + t : k * tiles + t + 1, :], (strip, 128))
                    factors.append(jnp.concatenate([f] * (tile // 128), axis=1).astype(BF16))

            def put(i, carry):
                first, second = strips[i, slot, 0], strips[i, slot, 1]
                for t in range(tiles):
                    weights[slot, pl.ds(pl.multiple_of(t * tile + i * strip, strip), strip), :] = (
                        first * factors[t] + second * factors[tiles + t]
                    )
                return carry

            lax.fori_loop(0, rows_of, put, 0)

    def masked(group, i):
        m = jnp.broadcast_to(maskv[group, pl.ds(i, 1), :], (16, width)).astype(BF16)
        a = both[group, pl.ds(pl.multiple_of(i * block, block), block), :]
        return (a.reshape(block // 16, 16, width) * m[None]).reshape(block, width)

    def coded(x):
        peak = jnp.maximum(jnp.max(jnp.abs(x), axis=0, keepdims=True), TINY)
        return jnp.round(x * (TOP / peak)).astype(jnp.int32).astype(LINK), peak * (1.0 / TOP)

    def rows(i):
        return pl.ds(pl.multiple_of(i * block, block), block)

    one_chip = 1 - 2 * y_lo * (1 - core)

    def flow_one(i):
        where = (r, at_chip(one_chip))
        return (
            pltpu.make_async_remote_copy(
                src_ref=s_out.at[rows(i)], dst_ref=r_one.at[rows(i)], send_sem=one_send.at[0, i],
                recv_sem=one_recv.at[0, i], device_id=where, device_id_type=MESH,
            ),
            pltpu.make_async_remote_copy(
                src_ref=s_scale.at[i], dst_ref=r_one_scale.at[i], send_sem=one_send.at[1, i],
                recv_sem=one_recv.at[1, i], device_id=where, device_id_type=MESH,
            ),
        )

    def flow_two(i):
        where = (r, at_chip(2))
        return (
            pltpu.make_async_remote_copy(
                src_ref=t_out.at[rows(i)], dst_ref=r_two.at[rows(i)], send_sem=two_send.at[0, i],
                recv_sem=two_recv.at[0, i], device_id=where, device_id_type=MESH,
            ),
            pltpu.make_async_remote_copy(
                src_ref=t_scale.at[i], dst_ref=r_two_scale.at[i], send_sem=two_send.at[1, i],
                recv_sem=two_recv.at[1, i], device_id=where, device_id_type=MESH,
            ),
        )

    ring_a = (p_a, ring_send_a, ring_recv_a)
    ring_b = (p_b, ring_send_b, ring_recv_b)
    for copy in shift_one:
        copy.wait_recv()
    cross_copy(*ring_a).start()
    for step in range(1, reach[0] + 2):
        ring_step(*ring_a, step)

    @pl.when(core == 0)
    def _():
        for copy in shift_two:
            copy.wait_recv()

    cross_copy(*ring_b).start()
    assemble(fac_a, p_a, w_a)
    own_amp.wait()
    for copy in swaps:
        copy.wait_recv()

    def outward(i, carry):
        x = jnp.dot(masked(0, i), w_a[0], preferred_element_type=F32)
        x = x + jnp.dot(masked(1, i), w_a[1], preferred_element_type=F32)
        code, scale = coded(x)
        s_out[rows(i)] = code
        s_scale[i] = jnp.broadcast_to(scale, (8, tile))
        for copy in flow_one(i):
            copy.start()
        return carry

    stages = reach[0] + 1
    done = 0
    for step in range(1, stages + 1):
        ring_step(*ring_b, step)
        upto = blocks * step // stages
        lax.fori_loop(done, upto, outward, 0)
        done = upto
    assemble(fac_b, p_b, w_b)

    def received(buf, scale, i):
        return buf[rows(i)].astype(jnp.int32).astype(F32) * scale[i][0:1]

    def inward(i, carry):
        m_even = jnp.dot(masked(0, i), w_b[0], preferred_element_type=F32)
        m_odd = jnp.dot(masked(1, i), w_b[1], preferred_element_type=F32)

        @pl.when(core == 1)
        def _():
            local[rows(i)] = m_even + m_odd

        @pl.when(core == 0)
        def _():
            local[rows(i)] = m_even
            t_own[...] = m_odd

            @pl.when(y_lo == 0)
            def _():
                for copy in flow_one(i):
                    copy.wait_recv()
                t_own[...] = t_own[...] + received(r_one, r_one_scale, i)

            code, scale = coded(t_own[...])
            t_out[rows(i)] = code
            t_scale[i] = jnp.broadcast_to(scale, (8, tile))
            for copy in flow_two(i):
                copy.start()

        return carry

    lax.fori_loop(0, blocks, inward, 0)

    def result_copy(i):
        return pltpu.make_async_copy(result.at[rows(i)], out.at[rows(i)], out_sem.at[i])

    def finish(i, carry):
        @pl.when(y_lo + core > 0)
        def _():
            for copy in flow_one(i):
                copy.wait_recv()
            local[rows(i)] = local[rows(i)] + received(r_one, r_one_scale, i)

        @pl.when(core == 0)
        def _():
            for copy in flow_two(i):
                copy.wait_recv()
            local[rows(i)] = local[rows(i)] + received(r_two, r_two_scale, i)

        result[rows(i)] = local[rows(i)].astype(BF16)
        result_copy(i).start()
        return carry

    lax.fori_loop(0, blocks, finish, 0)

    def drain_pieces(d, carry):
        for copy in piece_copies(d):
            copy.wait_send()
        return carry

    lax.fori_loop(1, rows_of, drain_pieces, 0)
    for copy in swaps + shift_one:
        copy.wait_send()

    @pl.when(core == 0)
    def _():
        for copy in shift_two:
            copy.wait_send()

    ring_drain(*ring_a)
    ring_drain(*ring_b)

    def drain_flows(i, carry):
        for copy in flow_one(i):
            copy.wait_send()

        @pl.when(core == 0)
        def _():
            for copy in flow_two(i):
                copy.wait_send()

        result_copy(i).wait()
        return carry

    lax.fori_loop(0, blocks, drain_flows, 0)


def shards(rows_of, cols_of, amplitudes, pair_mask, integrals, tile_list, tile_count, owner):
    count, width = amplitudes.shape
    tile = integrals.shape[-1]
    blocks, tiles = pair_mask.shape
    block = count // blocks
    strip = tile // rows_of
    reach = rows_of // 4
    dma = pltpu.SemaphoreType.DMA
    vmem = pltpu.VMEM
    smem = pl.BlockSpec(memory_space=pltpu.SMEM)
    away = pl.BlockSpec(memory_space=pl.ANY)
    code = vmem((count, tile), LINK)
    scale = vmem((blocks, 8, tile), F32)
    strips = vmem((rows_of, 2, 2, strip, tile), BF16)
    return pl.pallas_call(
        functools.partial(kernel, rows_of, cols_of),
        out_shape=jax.ShapeDtypeStruct((count, tile), BF16),
        in_specs=[smem, smem, smem, smem, away, away],
        out_specs=away,
        scratch_shapes=[
            vmem((2, count, width), BF16),
            vmem((2, blocks, width), F32),
            vmem((8, 128), F32),
            vmem((rows_of, 8, 128), F32),
            vmem((rows_of, 2, strip, tile), BF16),
            vmem((3, 8, 128), F32),
            vmem((2, 8, 128), F32),
            vmem((2, 8, 128), F32),
            vmem((3, 2, strip, tile), BF16),
            strips,
            strips,
            vmem((2, width, tile), BF16),
            vmem((2, width, tile), BF16),
            vmem((count, tile), F32),
            vmem((block, tile), F32),
            code, scale, code, scale, code, scale, code, scale,
            vmem((count, tile), BF16),
            dma((2,)), dma((2,)), dma((2,)),
            dma((2, rows_of)), dma((2, rows_of)),
            dma((4,)), dma((4,)),
            dma((2, 2, reach + 1)), dma((2, 2, reach + 1)),
            dma((2, 2, reach + 1)), dma((2, 2, reach + 1)),
            dma((2, blocks)), dma((2, blocks)),
            dma((2, blocks)), dma((2, blocks)),
            dma((blocks,)),
        ],
        compiler_params=pltpu.CompilerParams(
            collective_id=0, has_side_effects=True, vmem_limit_bytes=56 * 1024 * 1024
        ),
    )(owner, tile_list, tile_count, pair_mask, amplitudes, integrals.reshape(integrals.shape[2:]))


def solution(mesh):
    return jax.shard_map(
        functools.partial(shards, mesh.shape["row"], mesh.shape["col"]),
        mesh=mesh,
        in_specs=(
            P("row", "col"),
            P("row", "col"),
            P("row", "col", None, None, None),
            P("row", "col", None),
            P("row", "col"),
            P(None, "col"),
        ),
        out_specs=P("row", "col"),
        check_vma=False,
    )
```

```python
import functools

import jax
import jax.numpy as jnp
from jax import lax
from jax.experimental import pallas as pl
from jax.experimental.pallas import tpu as pltpu
from jax.sharding import PartitionSpec as P

MESH = pl.DeviceIdType.MESH
F32 = jnp.float32
BF16 = jnp.bfloat16
LINK = jnp.int16
TOP = 32767.0
TINY = 1e-33
AHEAD = 2
LAG = 4


def kernel(
    rows_of, cols_of, owner_ref, list_ref, count_ref, mask_ref, amp, panel, out,
    both, maskv, ahead, mask_ahead, meta, meta_in, piece_in, half_s, half_f, got_s, got_f, fac_a, fac_t, fac_l, fac_c,
    p_a, p_t, p_l, p_c, w_a, w_t, w_l, w_c, local, t_own, s_out, s_scale, r_one, r_one_scale, t_out, t_scale, r_two, r_two_scale, result,
    amp_sem, amp_send, amp_recv, ahead_send, ahead_recv, pass_send, pass_recv,
    a2a_send, a2a_recv, shift_send, shift_recv, ring_send, ring_recv, one_send, one_recv, two_send, two_recv, out_sem,
):
    r, c = lax.axis_index("row"), lax.axis_index("col")
    depth_z = rows_of // 2
    chips = cols_of // 2
    y, z = r // depth_z, r % depth_z
    chip, core = c // 2, c % 2
    y_lo = chip % 2
    tile = panel.shape[-1]
    strip = tile // depth_z
    blocks, tiles = mask_ref.shape
    block = amp.shape[0] // blocks
    width = amp.shape[1]

    def at_chip(step, same_core=True):
        return lax.rem(chip + step + chips, chips) * 2 + core

    row_id = lax.broadcasted_iota(jnp.int32, (8, 128), 0)
    flags = jnp.zeros((8, 128), F32)
    for k in range(2):
        live = jnp.where(k < count_ref[0, 0], k * tiles + list_ref[0, 0, k], -1)
        flags = flags + jnp.where(row_id == live, 1.0, 0.0)
    meta[...] = flags
    meta_in[z] = flags
    for t in range(tiles):
        maskv[core, :, t * tile : (t + 1) * tile] = jnp.broadcast_to(
            mask_ref[:, t : t + 1].astype(F32), (blocks, tile)
        )

    own_amp = pltpu.make_async_copy(amp, both.at[core], amp_sem.at[0])
    own_amp.start()
    own_piece = pltpu.make_async_copy(
        panel.at[:, pl.ds(pl.multiple_of(z * strip, strip), strip), :], piece_in.at[z], amp_sem.at[1]
    )
    own_piece.start()

    barrier = pltpu.get_barrier_semaphore()

    across = lax.rem(r + depth_z, rows_of)

    def z_peer(d):
        return lax.rem(z + d, depth_z)

    def greet(d, carry):
        pl.semaphore_signal(barrier, 1, device_id=(y * depth_z + z_peer(d), c), device_id_type=MESH)
        return carry

    lax.fori_loop(1, depth_z, greet, 0)
    for step in (1, -1, 2, -2):
        for row in (r, across):
            pl.semaphore_signal(barrier, 1, device_id=(row, at_chip(step)), device_id_type=MESH)
    partner = chip * 2 + 1 - core
    pl.semaphore_signal(barrier, 1, device_id=(across, c), device_id_type=MESH)
    pl.semaphore_signal(barrier, 1, device_id=(r, partner), device_id_type=MESH)
    pl.semaphore_wait(barrier, depth_z - 1 + 10)

    def piece_copies(d):
        peer = z_peer(d)
        return (
            pltpu.make_async_remote_copy(
                src_ref=panel.at[:, pl.ds(pl.multiple_of(peer * strip, strip), strip), :],
                dst_ref=piece_in.at[z],
                send_sem=a2a_send.at[0, d],
                recv_sem=a2a_recv.at[0, d],
                device_id=(y * depth_z + peer, c),
                device_id_type=MESH,
            ),
            pltpu.make_async_remote_copy(
                src_ref=meta,
                dst_ref=meta_in.at[z],
                send_sem=a2a_send.at[1, d],
                recv_sem=a2a_recv.at[1, d],
                device_id=(y * depth_z + peer, c),
                device_id_type=MESH,
            ),
        )

    def send_pieces(d, carry):
        for copy in piece_copies(d):
            copy.start()
        return carry

    lax.fori_loop(1, depth_z, send_pieces, 0)

    swaps = (
        pltpu.make_async_remote_copy(
            src_ref=maskv.at[core], dst_ref=maskv.at[core], send_sem=amp_send.at[0], recv_sem=amp_recv.at[0],
            device_id=(r, partner), device_id_type=MESH,
        ),
        pltpu.make_async_remote_copy(
            src_ref=amp, dst_ref=both.at[core], send_sem=amp_send.at[1], recv_sem=amp_recv.at[1],
            device_id=(r, partner), device_id_type=MESH,
        ),
    )
    for copy in swaps:
        copy.start()

    def rows(i):
        return pl.ds(pl.multiple_of(i * block, block), block)

    def ahead_copy(i):
        return pltpu.make_async_remote_copy(
            src_ref=amp.at[rows(i)], dst_ref=ahead.at[core, rows(i)], send_sem=ahead_send.at[i], recv_sem=ahead_recv.at[i],
            device_id=(r, at_chip(1)), device_id_type=MESH,
        )

    def pass_copy(i):
        return pltpu.make_async_remote_copy(
            src_ref=ahead.at[core, rows(i)], dst_ref=ahead.at[core, rows(i)], send_sem=pass_send.at[i],
            recv_sem=pass_recv.at[i], device_id=(r, partner), device_id_type=MESH,
        )

    mask_copy = pltpu.make_async_remote_copy(
        src_ref=maskv.at[core], dst_ref=mask_ahead.at[core], send_sem=ahead_send.at[AHEAD], recv_sem=ahead_recv.at[AHEAD],
        device_id=(r, at_chip(1)), device_id_type=MESH,
    )
    mask_pass = pltpu.make_async_remote_copy(
        src_ref=mask_ahead.at[core], dst_ref=mask_ahead.at[core], send_sem=pass_send.at[AHEAD],
        recv_sem=pass_recv.at[AHEAD], device_id=(r, partner), device_id_type=MESH,
    )
    mask_copy.start()
    ahead_copy(0).start()

    def wait_pieces(d, carry):
        for copy in piece_copies(d):
            copy.wait_recv()
        return carry

    own_piece.wait()
    lax.fori_loop(1, depth_z, wait_pieces, 0)

    def chosen(even_step, odd_step):
        holder = owner_ref[pl.ds(even_step * (1 - core) + odd_step * core, 1), :] - y * depth_z
        wide = jnp.broadcast_to(holder, (strip, tile))
        small = jnp.broadcast_to(holder, (8, 128))
        first, second, factors = jnp.zeros((strip, tile), BF16), jnp.zeros((strip, tile), BF16), jnp.zeros((8, 128), F32)
        for j in range(depth_z):
            named = jnp.where(wide == j, 1.0, 0.0).astype(BF16)
            first = first + named * piece_in[j, 0]
            second = second + named * piece_in[j, 1]
            factors = factors + jnp.where(small == j, meta_in[j], 0.0)
        return first, second, factors

    for slot, steps in enumerate(((2, 3), (1, 2), (0, 1), (3, 0))):
        half_s[slot, 0], half_s[slot, 1], half_f[slot] = chosen(*steps)

    def halves(first, count, landing, step, n):
        out = []
        for m, row in enumerate((r, across)):
            for k, (src, dst) in enumerate(((half_s, got_s), (half_f, got_f))):
                out.append(
                    pltpu.make_async_remote_copy(
                        src_ref=src.at[pl.ds(first, count)], dst_ref=dst.at[m, pl.ds(landing, count)],
                        send_sem=shift_send.at[n, m, k], recv_sem=shift_recv.at[n, m, k],
                        device_id=(row, at_chip(step)), device_id_type=MESH,
                    )
                )
        return out

    back_one = halves(0, 2, 0, -1, 0)
    stay = halves(0, 3, 2, 0, 1)[2:]
    stay_odd = halves(3, 1, 5, 0, 2)[2:]
    back_two = halves(3, 1, 5, -2, 2)
    for copy in back_one:
        copy.start()

    @pl.when(core == 0)
    def _():
        for copy in back_two:
            copy.start()

    for copy in stay:
        copy.start()

    @pl.when(core == 1)
    def _():
        for copy in stay_odd:
            copy.start()

    turn = 1 - 2 * core
    hops = [(0, 1), (0, -1)]
    if depth_z > 4:
        hops += [(0, 2), (0, -2), (2, 1), (-2, -1), (2 * turn, 2 * turn)]
    else:
        hops += [(0, 2 * turn)]
    direct = 4 if depth_z > 4 else 3

    def strips_of(which, back):
        return (p_a, p_t, p_l, p_c)[which].at[lax.rem(z - back + depth_z, depth_z)]

    def hop_copy(which, n):
        behind, on = hops[n]
        held = strips_of(which, behind)
        return pltpu.make_async_remote_copy(
            src_ref=held, dst_ref=held, send_sem=ring_send.at[which, n], recv_sem=ring_recv.at[which, n],
            device_id=(y * depth_z + lax.rem(z + on + depth_z, depth_z), c), device_id_type=MESH,
        )

    def hop_received(which, n):
        behind, on = hops[n]
        held = strips_of(which, behind + on)
        pltpu.make_async_remote_copy(
            src_ref=held, dst_ref=held, send_sem=ring_send.at[which, n], recv_sem=ring_recv.at[which, n],
            device_id=(r, partner), device_id_type=MESH,
        ).wait_recv()

    def ring_first(which):
        for n in range(direct):
            hop_copy(which, n).start()

    def ring_second(which):
        if direct < len(hops):
            hop_received(which, 2)
            hop_received(which, 3)
        for n in range(direct, len(hops)):
            hop_copy(which, n).start()

    def ring_rest(which):
        for n in range(len(hops)):
            if direct == len(hops) or n not in (2, 3):
                hop_received(which, n)

    def ring_drain(which):
        for n in range(len(hops)):
            hop_copy(which, n).wait_send()

    def assemble(fac, strips, weights):
        for slot in range(weights.shape[0]):
            factors = []
            for k in range(2):
                for t in range(tiles):
                    f = jnp.broadcast_to(fac[slot, k * tiles + t : k * tiles + t + 1, :], (strip, 128))
                    factors.append(jnp.concatenate([f] * (tile // 128), axis=1).astype(BF16))

            def put(i, carry):
                first, second = strips[i, slot, 0], strips[i, slot, 1]
                for t in range(tiles):
                    weights[slot, pl.ds(pl.multiple_of(t * tile + i * strip, strip), strip), :] = (
                        first * factors[t] + second * factors[tiles + t]
                    )
                return carry

            lax.fori_loop(0, depth_z, put, 0)

    def masked(group, i, mask=maskv, held=both):
        m = jnp.broadcast_to(mask[group, pl.ds(i, 1), :], (16, width)).astype(BF16)
        a = held[group, rows(i), :]
        return (a.reshape(block // 16, 16, width) * m[None]).reshape(block, width)

    def coded(x):
        peak = jnp.maximum(jnp.max(jnp.abs(x), axis=0, keepdims=True), TINY)
        return jnp.round(x * (TOP / peak)).astype(jnp.int32).astype(LINK), peak * (1.0 / TOP)

    one_chip = 1 - 2 * y_lo * (1 - core)

    def flow_one(i):
        where = (r, at_chip(one_chip))
        return (
            pltpu.make_async_remote_copy(
                src_ref=s_out.at[rows(i)], dst_ref=r_one.at[rows(i)], send_sem=one_send.at[0, i],
                recv_sem=one_recv.at[0, i], device_id=where, device_id_type=MESH,
            ),
            pltpu.make_async_remote_copy(
                src_ref=s_scale.at[i], dst_ref=r_one_scale.at[i], send_sem=one_send.at[1, i],
                recv_sem=one_recv.at[1, i], device_id=where, device_id_type=MESH,
            ),
        )

    def flow_two(i):
        where = (r, at_chip(2))
        return (
            pltpu.make_async_remote_copy(
                src_ref=t_out.at[rows(i)], dst_ref=r_two.at[rows(i)], send_sem=two_send.at[0, i],
                recv_sem=two_recv.at[0, i], device_id=where, device_id_type=MESH,
            ),
            pltpu.make_async_remote_copy(
                src_ref=t_scale.at[i], dst_ref=r_two_scale.at[i], send_sem=two_send.at[1, i],
                recv_sem=two_recv.at[1, i], device_id=where, device_id_type=MESH,
            ),
        )

    for copy in back_one:
        copy.wait_recv()
    for slot in (0, 1):
        p_a[z, slot] = got_s[0, slot] + got_s[1, slot]
        fac_a[slot] = got_f[0, slot] + got_f[1, slot]
    ring_first(0)

    @pl.when(core == 0)
    def _():
        for copy in back_two:
            copy.wait_recv()
        p_t[z, 0] = got_s[0, 5] + got_s[1, 5]
        fac_t[0] = got_f[0, 5] + got_f[1, 5]

    @pl.when(core == 1)
    def _():
        for copy in stay_odd:
            copy.wait_recv()
        p_t[z, 0] = half_s[3] + got_s[1, 5]
        fac_t[0] = half_f[3] + got_f[1, 5]

    for copy in stay:
        copy.wait_recv()
    for i in range(1, AHEAD):
        ahead_copy(i).start()
    p_l[z, 0] = half_s[2] + got_s[1, 4]
    fac_l[0] = half_f[2] + got_f[1, 4]
    for slot in (0, 1):
        p_c[z, slot] = half_s[slot] + got_s[1, 2 + slot]
        fac_c[slot] = half_f[slot] + got_f[1, 2 + slot]
    ring_second(0)
    ring_first(1)
    ring_rest(0)
    assemble(fac_a, p_a, w_a)
    own_amp.wait()
    for copy in swaps:
        copy.wait_recv()

    def outward(i):
        x = jnp.dot(masked(0, i), w_a[0], preferred_element_type=F32)
        x = x + jnp.dot(masked(1, i), w_a[1], preferred_element_type=F32)
        code, scale = coded(x)
        s_out[rows(i)] = code
        s_scale[i] = jnp.broadcast_to(scale, (8, tile))
        for copy in flow_one(i):
            copy.start()

    def received(buf, scale, i):
        return buf[rows(i)].astype(jnp.int32).astype(F32) * scale[i][0:1]

    def send_two(i, x):
        code, scale = coded(x)
        t_out[rows(i)] = code
        t_scale[i] = jnp.broadcast_to(scale, (8, tile))
        for copy in flow_two(i):
            copy.start()

    def odd_term(i, direct):
        x = jnp.dot(masked(1, i), w_t[0], preferred_element_type=F32)
        t_own[rows(i)] = x

        @pl.when((core == 0) if direct else ((core == 0) & (y_lo == 1)))
        def _():
            send_two(i, x)

    def relay(i):
        @pl.when((core == 0) & (y_lo == 0))
        def _():
            for copy in flow_one(i):
                copy.wait_recv()
            send_two(i, t_own[rows(i)] + received(r_one, r_one_scale, i))

    def result_copy(i):
        return pltpu.make_async_copy(result.at[rows(i)], out.at[rows(i)], out_sem.at[i])

    def here(i):
        x = jnp.dot(masked(0, i), w_l[0], preferred_element_type=F32)

        @pl.when(core == 1)
        def _():
            local[rows(i)] = x + t_own[rows(i)]

        @pl.when(core == 0)
        def _():
            local[rows(i)] = x

    def finish(i, early):
        if not early:

            @pl.when(y_lo + core > 0)
            def _():
                for copy in flow_one(i):
                    copy.wait_recv()
                local[rows(i)] = local[rows(i)] + received(r_one, r_one_scale, i)

        @pl.when(core == 0)
        def _():
            for copy in flow_two(i):
                copy.wait_recv()
            local[rows(i)] = local[rows(i)] + received(r_two, r_two_scale, i)

        result[rows(i)] = local[rows(i)].astype(BF16)
        result_copy(i).start()

    def each(first, last, *calls):
        def body(i, carry):
            for call in calls:
                call(i)
            return carry

        lax.fori_loop(first, last, body, 0)

    late = blocks - AHEAD
    cuts = [AHEAD + late * k // 4 for k in range(5)]
    each(cuts[0], cuts[1], outward)
    ring_second(1)
    for which in (2, 3):
        ring_first(which)
    each(cuts[1], cuts[2], outward)
    ring_rest(1)
    assemble(fac_t, p_t, w_t)
    each(0, AHEAD, lambda i: odd_term(i, True))
    each(cuts[0], cuts[1], lambda i: odd_term(i, False))
    each(cuts[2], cuts[3], outward)
    for which in (2, 3):
        ring_second(which)
    each(cuts[1], cuts[2], lambda i: odd_term(i, False))
    each(cuts[3], cuts[4], outward)
    mask_copy.wait_recv()
    mask_pass.start()
    for i in range(AHEAD):
        ahead_copy(i).wait_recv()
        pass_copy(i).start()
    each(cuts[2], cuts[4], lambda i: odd_term(i, False))
    each(cuts[0], cuts[1], relay)
    ring_rest(2)
    assemble(fac_l, p_l, w_l)
    each(0, blocks, here)
    each(cuts[1], cuts[2], relay)
    ring_rest(3)
    assemble(fac_c, p_c, w_c)
    mask_pass.wait_recv()

    def from_ahead(i):
        pass_copy(i).wait_recv()
        local[rows(i)] = (
            local[rows(i)]
            + jnp.dot(masked(0, i, mask_ahead, ahead), w_c[0], preferred_element_type=F32)
            + jnp.dot(masked(1, i, mask_ahead, ahead), w_c[1], preferred_element_type=F32)
        )
        finish(i, True)

    each(0, AHEAD, from_ahead)
    ready = cuts[2] - LAG
    assert ready >= AHEAD
    each(AHEAD, ready, lambda i: finish(i, False))
    each(cuts[2], blocks, relay, lambda i: finish(i - LAG, False))
    each(blocks - LAG, blocks, lambda i: finish(i, False))

    def drain_pieces(d, carry):
        for copy in piece_copies(d):
            copy.wait_send()
        return carry

    lax.fori_loop(1, depth_z, drain_pieces, 0)
    for copy in list(swaps) + back_one + stay:
        copy.wait_send()

    @pl.when(core == 0)
    def _():
        for copy in back_two:
            copy.wait_send()

    @pl.when(core == 1)
    def _():
        for copy in stay_odd:
            copy.wait_send()

    for which in (0, 1, 2, 3):
        ring_drain(which)
    for copy in (mask_copy, mask_pass):
        copy.wait_send()
    for i in range(AHEAD):
        ahead_copy(i).wait_send()
        pass_copy(i).wait_send()

    def drain_one(i, carry):
        for copy in flow_one(i):
            copy.wait_send()
        return carry

    lax.fori_loop(AHEAD, blocks, drain_one, 0)

    def drain_two(i, carry):
        @pl.when(core == 0)
        def _():
            for copy in flow_two(i):
                copy.wait_send()

        result_copy(i).wait()
        return carry

    lax.fori_loop(0, blocks, drain_two, 0)


def shards(rows_of, cols_of, amplitudes, pair_mask, integrals, tile_list, tile_count, owner):
    count, width = amplitudes.shape
    tile = integrals.shape[-1]
    blocks, tiles = pair_mask.shape
    block = count // blocks
    depth_z = rows_of // 2
    strip = tile // depth_z
    hops = 7 if depth_z > 4 else 3
    dma = pltpu.SemaphoreType.DMA
    vmem = pltpu.VMEM
    near = pl.BlockSpec(memory_space=pltpu.VMEM)
    smem = pl.BlockSpec(memory_space=pltpu.SMEM)
    away = pl.BlockSpec(memory_space=pl.ANY)
    code = vmem((count, tile), LINK)
    scale = vmem((blocks, 8, tile), F32)

    def strips(slots):
        return vmem((depth_z, slots, 2, strip, tile), BF16)

    return pl.pallas_call(
        functools.partial(kernel, rows_of, cols_of),
        out_shape=jax.ShapeDtypeStruct((count, tile), BF16),
        in_specs=[near, smem, smem, near, away, away],
        out_specs=away,
        scratch_shapes=[
            vmem((2, count, width), BF16),
            vmem((2, blocks, width), F32),
            vmem((2, AHEAD * block, width), BF16),
            vmem((2, blocks, width), F32),
            vmem((8, 128), F32),
            vmem((depth_z, 8, 128), F32),
            vmem((depth_z, 2, strip, tile), BF16),
            vmem((4, 2, strip, tile), BF16),
            vmem((4, 8, 128), F32),
            vmem((2, 6, 2, strip, tile), BF16),
            vmem((2, 6, 8, 128), F32),
            vmem((2, 8, 128), F32),
            vmem((1, 8, 128), F32),
            vmem((1, 8, 128), F32),
            vmem((2, 8, 128), F32),
            strips(2), strips(1), strips(1), strips(2),
            vmem((2, width, tile), BF16),
            vmem((1, width, tile), BF16),
            vmem((1, width, tile), BF16),
            vmem((2, width, tile), BF16),
            vmem((count, tile), F32),
            vmem((count, tile), F32),
            code, scale, code, scale, code, scale, code, scale,
            vmem((count, tile), BF16),
            dma((2,)), dma((2,)), dma((2,)),
            dma((AHEAD + 1,)), dma((AHEAD + 1,)), dma((AHEAD + 1,)), dma((AHEAD + 1,)),
            dma((2, depth_z)), dma((2, depth_z)),
            dma((3, 2, 2)), dma((3, 2, 2)),
            dma((4, hops)), dma((4, hops)),
            dma((2, blocks)), dma((2, blocks)),
            dma((2, blocks)), dma((2, blocks)),
            dma((blocks,)),
        ],
        compiler_params=pltpu.CompilerParams(
            collective_id=0, has_side_effects=True, vmem_limit_bytes=56 * 1024 * 1024
        ),
    )(owner, tile_list, tile_count, pair_mask, amplitudes, integrals.reshape(integrals.shape[2:]))


def solution(mesh):
    return jax.shard_map(
        functools.partial(shards, mesh.shape["row"], mesh.shape["col"]),
        mesh=mesh,
        in_specs=(
            P("row", "col"),
            P("row", "col"),
            P("row", "col", None, None, None),
            P("row", "col", None),
            P("row", "col"),
            P(None, "col"),
        ),
        out_specs=P("row", "col"),
        check_vma=False,
    )
```

```python
import functools

import jax
import jax.numpy as jnp
from jax import lax
from jax.experimental import pallas as pl
from jax.experimental.pallas import tpu as pltpu
from jax.sharding import PartitionSpec as P

MESH = pl.DeviceIdType.MESH
F32 = jnp.float32
BF16 = jnp.bfloat16
LINK = jnp.int16
TOP = 32767.0
TINY = 1e-33
AHEAD = 2
EARLY = 2
LAG = 4


def kernel(
    rows_of, cols_of, owner_ref, list_ref, count_ref, mask_ref, amp, panel, out,
    both, maskv, ahead, mask_ahead, meta, meta_in, piece_in, half_s, half_f, got_s, got_f, fac_a, fac_t, fac_l, fac_c,
    p_a, p_t, p_l, p_c, w_a, w_t, w_l, w_c, local, t_own, s_out, s_scale, r_one, r_one_scale, t_out, t_scale, r_two, r_two_scale, result,
    amp_sem, amp_send, amp_recv, ahead_send, ahead_recv, pass_send, pass_recv,
    a2a_send, a2a_recv, shift_send, shift_recv, ring_send, ring_recv, one_send, one_recv, two_send, two_recv, out_sem,
):
    r, c = lax.axis_index("row"), lax.axis_index("col")
    depth_z = rows_of // 2
    chips = cols_of // 2
    y, z = r // depth_z, r % depth_z
    chip, core = c // 2, c % 2
    y_lo = chip % 2
    tile = panel.shape[-1]
    strip = tile // depth_z
    blocks, tiles = mask_ref.shape
    block = amp.shape[0] // blocks
    width = amp.shape[1]

    def at_chip(step, same_core=True):
        return lax.rem(chip + step + chips, chips) * 2 + core

    row_id = lax.broadcasted_iota(jnp.int32, (8, 128), 0)
    flags = jnp.zeros((8, 128), F32)
    for k in range(2):
        live = jnp.where(k < count_ref[0, 0], k * tiles + list_ref[0, 0, k], -1)
        flags = flags + jnp.where(row_id == live, 1.0, 0.0)
    meta[...] = flags
    meta_in[z] = flags
    for t in range(tiles):
        maskv[core, :, t * tile : (t + 1) * tile] = jnp.broadcast_to(
            mask_ref[:, t : t + 1].astype(F32), (blocks, tile)
        )

    own_amp = pltpu.make_async_copy(amp, both.at[core], amp_sem.at[0])
    own_amp.start()
    own_piece = pltpu.make_async_copy(
        panel.at[:, pl.ds(pl.multiple_of(z * strip, strip), strip), :], piece_in.at[z], amp_sem.at[1]
    )
    own_piece.start()

    barrier = pltpu.get_barrier_semaphore()

    across = lax.rem(r + depth_z, rows_of)

    def z_peer(d):
        return lax.rem(z + d, depth_z)

    def greet(d, carry):
        pl.semaphore_signal(barrier, 1, device_id=(y * depth_z + z_peer(d), c), device_id_type=MESH)
        return carry

    lax.fori_loop(1, depth_z, greet, 0)
    for step in (1, -1, 2, -2):
        for row in (r, across):
            pl.semaphore_signal(barrier, 1, device_id=(row, at_chip(step)), device_id_type=MESH)
    partner = chip * 2 + 1 - core
    pl.semaphore_signal(barrier, 1, device_id=(across, c), device_id_type=MESH)
    pl.semaphore_signal(barrier, 1, device_id=(r, partner), device_id_type=MESH)
    pl.semaphore_wait(barrier, depth_z - 1 + 10)

    def piece_copies(d):
        peer = z_peer(d)
        return (
            pltpu.make_async_remote_copy(
                src_ref=panel.at[:, pl.ds(pl.multiple_of(peer * strip, strip), strip), :],
                dst_ref=piece_in.at[z],
                send_sem=a2a_send.at[0, d],
                recv_sem=a2a_recv.at[0, d],
                device_id=(y * depth_z + peer, c),
                device_id_type=MESH,
            ),
            pltpu.make_async_remote_copy(
                src_ref=meta,
                dst_ref=meta_in.at[z],
                send_sem=a2a_send.at[1, d],
                recv_sem=a2a_recv.at[1, d],
                device_id=(y * depth_z + peer, c),
                device_id_type=MESH,
            ),
        )

    def send_pieces(d, carry):
        for copy in piece_copies(d):
            copy.start()
        return carry

    lax.fori_loop(1, depth_z, send_pieces, 0)

    swaps = (
        pltpu.make_async_remote_copy(
            src_ref=maskv.at[core], dst_ref=maskv.at[core], send_sem=amp_send.at[0], recv_sem=amp_recv.at[0],
            device_id=(r, partner), device_id_type=MESH,
        ),
        pltpu.make_async_remote_copy(
            src_ref=amp, dst_ref=both.at[core], send_sem=amp_send.at[1], recv_sem=amp_recv.at[1],
            device_id=(r, partner), device_id_type=MESH,
        ),
    )
    for copy in swaps:
        copy.start()

    def rows(i):
        return pl.ds(pl.multiple_of(i * block, block), block)

    def half_rows(n):
        return pl.ds(pl.multiple_of(n * (block // 2), block // 2), block // 2)

    def ahead_copy(n):
        return pltpu.make_async_remote_copy(
            src_ref=amp.at[half_rows(n)], dst_ref=ahead.at[core, half_rows(n)], send_sem=ahead_send.at[n],
            recv_sem=ahead_recv.at[n], device_id=(r, at_chip(1)), device_id_type=MESH,
        )

    def pass_copy(n):
        return pltpu.make_async_remote_copy(
            src_ref=ahead.at[core, half_rows(n)], dst_ref=ahead.at[core, half_rows(n)], send_sem=pass_send.at[n],
            recv_sem=pass_recv.at[n], device_id=(r, partner), device_id_type=MESH,
        )

    mask_copy = pltpu.make_async_remote_copy(
        src_ref=maskv.at[core], dst_ref=mask_ahead.at[core], send_sem=ahead_send.at[2 * AHEAD], recv_sem=ahead_recv.at[2 * AHEAD],
        device_id=(r, at_chip(1)), device_id_type=MESH,
    )
    mask_pass = pltpu.make_async_remote_copy(
        src_ref=mask_ahead.at[core], dst_ref=mask_ahead.at[core], send_sem=pass_send.at[2 * AHEAD],
        recv_sem=pass_recv.at[2 * AHEAD], device_id=(r, partner), device_id_type=MESH,
    )
    mask_copy.start()
    for n in range(EARLY):
        ahead_copy(n).start()

    def wait_pieces(d, carry):
        for copy in piece_copies(d):
            copy.wait_recv()
        return carry

    own_piece.wait()
    lax.fori_loop(1, depth_z, wait_pieces, 0)

    def chosen(even_step, odd_step):
        holder = owner_ref[pl.ds(even_step * (1 - core) + odd_step * core, 1), :] - y * depth_z
        wide = jnp.broadcast_to(holder, (strip, tile))
        small = jnp.broadcast_to(holder, (8, 128))
        first, second, factors = jnp.zeros((strip, tile), BF16), jnp.zeros((strip, tile), BF16), jnp.zeros((8, 128), F32)
        for j in range(depth_z):
            named = jnp.where(wide == j, 1.0, 0.0).astype(BF16)
            first = first + named * piece_in[j, 0]
            second = second + named * piece_in[j, 1]
            factors = factors + jnp.where(small == j, meta_in[j], 0.0)
        return first, second, factors

    for slot, steps in enumerate(((2, 3), (1, 2), (0, 1), (3, 0))):
        half_s[slot, 0], half_s[slot, 1], half_f[slot] = chosen(*steps)

    def halves(first, count, landing, step, n):
        out = []
        for m, row in enumerate((r, across)):
            for k, (src, dst) in enumerate(((half_s, got_s), (half_f, got_f))):
                out.append(
                    pltpu.make_async_remote_copy(
                        src_ref=src.at[pl.ds(first, count)], dst_ref=dst.at[m, pl.ds(landing, count)],
                        send_sem=shift_send.at[n, m, k], recv_sem=shift_recv.at[n, m, k],
                        device_id=(row, at_chip(step)), device_id_type=MESH,
                    )
                )
        return out

    back_one = (halves(0, 1, 0, -1, 0), halves(1, 1, 1, -1, 3))
    stay = halves(0, 3, 2, 0, 1)[2:]
    stay_odd = halves(3, 1, 5, 0, 2)[2:]
    back_two = halves(3, 1, 5, -2, 2)
    for copy in back_one[0] + back_one[1]:
        copy.start()

    @pl.when(core == 0)
    def _():
        for copy in back_two:
            copy.start()

    for copy in stay:
        copy.start()

    @pl.when(core == 1)
    def _():
        for copy in stay_odd:
            copy.start()

    turn = 1 - 2 * core
    if depth_z > 4:
        hops = [(0, 2), (0, -2), (0, 1), (0, -1), (2, 1), (-2, -1), (2 * turn, 2 * turn)]
    else:
        hops = [(0, 2 * turn), (0, 1), (0, -1)]
    direct = 4 if depth_z > 4 else 3

    def strips_of(which, back):
        buf, slot = ((p_a, 0), (p_a, 1), (p_t, 0), (p_l, 0), (p_c, 0), (p_c, 1))[which]
        return buf.at[lax.rem(z - back + depth_z, depth_z), slot]

    def hop_copy(which, n):
        behind, on = hops[n]
        held = strips_of(which, behind)
        return pltpu.make_async_remote_copy(
            src_ref=held, dst_ref=held, send_sem=ring_send.at[which, n], recv_sem=ring_recv.at[which, n],
            device_id=(y * depth_z + lax.rem(z + on + depth_z, depth_z), c), device_id_type=MESH,
        )

    def hop_received(which, n):
        behind, on = hops[n]
        held = strips_of(which, behind + on)
        pltpu.make_async_remote_copy(
            src_ref=held, dst_ref=held, send_sem=ring_send.at[which, n], recv_sem=ring_recv.at[which, n],
            device_id=(r, partner), device_id_type=MESH,
        ).wait_recv()

    def ring_first(which):
        for n in range(direct):
            hop_copy(which, n).start()

    def ring_second(which):
        if direct < len(hops):
            hop_received(which, 0)
            hop_received(which, 1)
        for n in range(direct, len(hops)):
            hop_copy(which, n).start()

    def ring_rest(which):
        for n in range(len(hops)):
            if direct == len(hops) or n not in (0, 1):
                hop_received(which, n)

    def ring_drain(which):
        for n in range(len(hops)):
            hop_copy(which, n).wait_send()

    def assemble(fac, strips, weights, *slots):
        for slot in slots:
            factors = []
            for k in range(2):
                for t in range(tiles):
                    f = jnp.broadcast_to(fac[slot, k * tiles + t : k * tiles + t + 1, :], (strip, 128))
                    factors.append(jnp.concatenate([f] * (tile // 128), axis=1).astype(BF16))

            def put(i, carry):
                first, second = strips[i, slot, 0], strips[i, slot, 1]
                for t in range(tiles):
                    weights[slot, pl.ds(pl.multiple_of(t * tile + i * strip, strip), strip), :] = (
                        first * factors[t] + second * factors[tiles + t]
                    )
                return carry

            lax.fori_loop(0, depth_z, put, 0)

    def masked(group, i, mask=maskv, held=both):
        m = jnp.broadcast_to(mask[group, pl.ds(i, 1), :], (16, width)).astype(BF16)
        a = held[group, rows(i), :]
        return (a.reshape(block // 16, 16, width) * m[None]).reshape(block, width)

    def coded(x):
        peak = jnp.maximum(jnp.max(jnp.abs(x), axis=0, keepdims=True), TINY)
        return jnp.round(x * (TOP / peak)).astype(jnp.int32).astype(LINK), peak * (1.0 / TOP)

    one_chip = 1 - 2 * y_lo * (1 - core)

    def flow_one(i):
        where = (r, at_chip(one_chip))
        return (
            pltpu.make_async_remote_copy(
                src_ref=s_out.at[rows(i)], dst_ref=r_one.at[rows(i)], send_sem=one_send.at[0, i],
                recv_sem=one_recv.at[0, i], device_id=where, device_id_type=MESH,
            ),
            pltpu.make_async_remote_copy(
                src_ref=s_scale.at[i, pl.ds(0, 1)], dst_ref=r_one_scale.at[i, pl.ds(0, 1)], send_sem=one_send.at[1, i],
                recv_sem=one_recv.at[1, i], device_id=where, device_id_type=MESH,
            ),
        )

    def flow_two(i):
        where = (r, at_chip(2))
        return (
            pltpu.make_async_remote_copy(
                src_ref=t_out.at[rows(i)], dst_ref=r_two.at[rows(i)], send_sem=two_send.at[0, i],
                recv_sem=two_recv.at[0, i], device_id=where, device_id_type=MESH,
            ),
            pltpu.make_async_remote_copy(
                src_ref=t_scale.at[i, pl.ds(0, 1)], dst_ref=r_two_scale.at[i, pl.ds(0, 1)], send_sem=two_send.at[1, i],
                recv_sem=two_recv.at[1, i], device_id=where, device_id_type=MESH,
            ),
        )

    for slot in (0, 1):
        for copy in back_one[slot]:
            copy.wait_recv()
        p_a[z, slot] = got_s[0, slot] + got_s[1, slot]
        fac_a[slot] = got_f[0, slot] + got_f[1, slot]
        ring_first(slot)
    ring_second(0)

    @pl.when(core == 0)
    def _():
        for copy in back_two:
            copy.wait_recv()
        p_t[z, 0] = got_s[0, 5] + got_s[1, 5]
        fac_t[0] = got_f[0, 5] + got_f[1, 5]

    @pl.when(core == 1)
    def _():
        for copy in stay_odd:
            copy.wait_recv()
        p_t[z, 0] = half_s[3] + got_s[1, 5]
        fac_t[0] = half_f[3] + got_f[1, 5]

    for copy in stay:
        copy.wait_recv()
    for n in range(EARLY, 2 * AHEAD):
        ahead_copy(n).start()
    p_l[z, 0] = half_s[2] + got_s[1, 4]
    fac_l[0] = half_f[2] + got_f[1, 4]
    for slot in (0, 1):
        p_c[z, slot] = half_s[slot] + got_s[1, 2 + slot]
        fac_c[slot] = half_f[slot] + got_f[1, 2 + slot]
    ring_second(1)
    ring_rest(0)
    assemble(fac_a, p_a, w_a, 0)
    ring_first(2)
    ring_rest(1)
    assemble(fac_a, p_a, w_a, 1)
    own_amp.wait()
    for copy in swaps:
        copy.wait_recv()

    def outward(i):
        x = jnp.dot(masked(0, i), w_a[0], preferred_element_type=F32)
        x = x + jnp.dot(masked(1, i), w_a[1], preferred_element_type=F32)
        code, scale = coded(x)
        s_out[rows(i)] = code
        s_scale[i, 0:1] = scale
        for copy in flow_one(i):
            copy.start()

    def received(buf, scale, i):
        return buf[rows(i)].astype(jnp.int32).astype(F32) * scale[i, 0:1]

    def send_two(i, x):
        code, scale = coded(x)
        t_out[rows(i)] = code
        t_scale[i, 0:1] = scale
        for copy in flow_two(i):
            copy.start()

    def odd_term(i, direct):
        x = jnp.dot(masked(1, i), w_t[0], preferred_element_type=F32)
        t_own[rows(i)] = x

        @pl.when((core == 0) if direct else ((core == 0) & (y_lo == 1)))
        def _():
            send_two(i, x)

    def relay(i):
        @pl.when((core == 0) & (y_lo == 0))
        def _():
            for copy in flow_one(i):
                copy.wait_recv()
            send_two(i, t_own[rows(i)] + received(r_one, r_one_scale, i))

    def result_copy(i):
        return pltpu.make_async_copy(result.at[rows(i)], out.at[rows(i)], out_sem.at[i])

    def here(i):
        x = jnp.dot(masked(0, i), w_l[0], preferred_element_type=F32)

        @pl.when(core == 1)
        def _():
            local[rows(i)] = x + t_own[rows(i)]

        @pl.when(core == 0)
        def _():
            local[rows(i)] = x

    def finish(i, early):
        if not early:

            @pl.when(y_lo + core > 0)
            def _():
                for copy in flow_one(i):
                    copy.wait_recv()
                local[rows(i)] = local[rows(i)] + received(r_one, r_one_scale, i)

        @pl.when(core == 0)
        def _():
            for copy in flow_two(i):
                copy.wait_recv()
            local[rows(i)] = local[rows(i)] + received(r_two, r_two_scale, i)

        result[rows(i)] = local[rows(i)].astype(BF16)
        result_copy(i).start()

    def each(first, last, *calls):
        def body(i, carry):
            for call in calls:
                call(i)
            return carry

        lax.fori_loop(first, last, body, 0)

    late = blocks - AHEAD
    cuts = [AHEAD + late * k // 4 for k in range(5)]
    each(cuts[0], cuts[1], outward)
    ring_second(2)
    for which in (3, 4, 5):
        ring_first(which)
    each(cuts[1], cuts[2], outward)
    ring_rest(2)
    assemble(fac_t, p_t, w_t, 0)
    each(0, AHEAD, lambda i: odd_term(i, True))
    each(cuts[0], cuts[1], lambda i: odd_term(i, False))
    each(cuts[2], cuts[3], outward)
    for which in (3, 4, 5):
        ring_second(which)
    each(cuts[1], cuts[2], lambda i: odd_term(i, False))
    each(cuts[3], cuts[4], outward)
    mask_copy.wait_recv()
    mask_pass.start()
    for n in range(2 * AHEAD):
        ahead_copy(n).wait_recv()
        pass_copy(n).start()
    each(cuts[2], cuts[4], lambda i: odd_term(i, False))
    each(cuts[0], cuts[1], relay)
    ring_rest(3)
    assemble(fac_l, p_l, w_l, 0)
    each(0, blocks, here)
    each(cuts[1], cuts[2], relay)
    ring_rest(4)
    ring_rest(5)
    assemble(fac_c, p_c, w_c, 0, 1)
    mask_pass.wait_recv()

    def from_ahead(i):
        pass_copy(2 * i).wait_recv()
        pass_copy(2 * i + 1).wait_recv()
        local[rows(i)] = (
            local[rows(i)]
            + jnp.dot(masked(0, i, mask_ahead, ahead), w_c[0], preferred_element_type=F32)
            + jnp.dot(masked(1, i, mask_ahead, ahead), w_c[1], preferred_element_type=F32)
        )
        finish(i, True)

    each(0, AHEAD, from_ahead)
    ready = cuts[2] - LAG
    assert ready >= AHEAD
    each(AHEAD, ready, lambda i: finish(i, False))
    each(cuts[2], blocks, relay, lambda i: finish(i - LAG, False))
    each(blocks - LAG, blocks, lambda i: finish(i, False))

    def drain_pieces(d, carry):
        for copy in piece_copies(d):
            copy.wait_send()
        return carry

    lax.fori_loop(1, depth_z, drain_pieces, 0)
    for copy in list(swaps) + back_one[0] + back_one[1] + stay:
        copy.wait_send()

    @pl.when(core == 0)
    def _():
        for copy in back_two:
            copy.wait_send()

    @pl.when(core == 1)
    def _():
        for copy in stay_odd:
            copy.wait_send()

    for which in range(6):
        ring_drain(which)
    for copy in (mask_copy, mask_pass):
        copy.wait_send()
    for n in range(2 * AHEAD):
        ahead_copy(n).wait_send()
        pass_copy(n).wait_send()

    def drain_one(i, carry):
        for copy in flow_one(i):
            copy.wait_send()
        return carry

    lax.fori_loop(AHEAD, blocks, drain_one, 0)

    def drain_two(i, carry):
        @pl.when(core == 0)
        def _():
            for copy in flow_two(i):
                copy.wait_send()

        result_copy(i).wait()
        return carry

    lax.fori_loop(0, blocks, drain_two, 0)


def shards(rows_of, cols_of, amplitudes, pair_mask, integrals, tile_list, tile_count, owner):
    count, width = amplitudes.shape
    tile = integrals.shape[-1]
    blocks, tiles = pair_mask.shape
    block = count // blocks
    depth_z = rows_of // 2
    strip = tile // depth_z
    hops = 7 if depth_z > 4 else 3
    dma = pltpu.SemaphoreType.DMA
    vmem = pltpu.VMEM
    near = pl.BlockSpec(memory_space=pltpu.VMEM)
    smem = pl.BlockSpec(memory_space=pltpu.SMEM)
    away = pl.BlockSpec(memory_space=pl.ANY)
    code = vmem((count, tile), LINK)
    scale = vmem((blocks, 8, tile), F32)

    def strips(slots):
        return vmem((depth_z, slots, 2, strip, tile), BF16)

    return pl.pallas_call(
        functools.partial(kernel, rows_of, cols_of),
        out_shape=jax.ShapeDtypeStruct((count, tile), BF16),
        in_specs=[near, smem, smem, near, away, away],
        out_specs=away,
        scratch_shapes=[
            vmem((2, count, width), BF16),
            vmem((2, blocks, width), F32),
            vmem((2, AHEAD * block, width), BF16),
            vmem((2, blocks, width), F32),
            vmem((8, 128), F32),
            vmem((depth_z, 8, 128), F32),
            vmem((depth_z, 2, strip, tile), BF16),
            vmem((4, 2, strip, tile), BF16),
            vmem((4, 8, 128), F32),
            vmem((2, 6, 2, strip, tile), BF16),
            vmem((2, 6, 8, 128), F32),
            vmem((2, 8, 128), F32),
            vmem((1, 8, 128), F32),
            vmem((1, 8, 128), F32),
            vmem((2, 8, 128), F32),
            strips(2), strips(1), strips(1), strips(2),
            vmem((2, width, tile), BF16),
            vmem((1, width, tile), BF16),
            vmem((1, width, tile), BF16),
            vmem((2, width, tile), BF16),
            vmem((count, tile), F32),
            vmem((count, tile), F32),
            code, scale, code, scale, code, scale, code, scale,
            vmem((count, tile), BF16),
            dma((2,)), dma((2,)), dma((2,)),
            dma((2 * AHEAD + 1,)), dma((2 * AHEAD + 1,)), dma((2 * AHEAD + 1,)), dma((2 * AHEAD + 1,)),
            dma((2, depth_z)), dma((2, depth_z)),
            dma((4, 2, 2)), dma((4, 2, 2)),
            dma((6, hops)), dma((6, hops)),
            dma((2, blocks)), dma((2, blocks)),
            dma((2, blocks)), dma((2, blocks)),
            dma((blocks,)),
        ],
        compiler_params=pltpu.CompilerParams(
            collective_id=0, has_side_effects=True, vmem_limit_bytes=56 * 1024 * 1024
        ),
    )(owner, tile_list, tile_count, pair_mask, amplitudes, integrals.reshape(integrals.shape[2:]))


def solution(mesh):
    return jax.shard_map(
        functools.partial(shards, mesh.shape["row"], mesh.shape["col"]),
        mesh=mesh,
        in_specs=(
            P("row", "col"),
            P("row", "col"),
            P("row", "col", None, None, None),
            P("row", "col", None),
            P("row", "col"),
            P(None, "col"),
        ),
        out_specs=P("row", "col"),
        check_vma=False,
    )
```

```python
import functools

import jax
import jax.numpy as jnp
from jax import lax
from jax.experimental import pallas as pl
from jax.experimental.pallas import tpu as pltpu
from jax.sharding import PartitionSpec as P

MESH = pl.DeviceIdType.MESH
F32 = jnp.float32
BF16 = jnp.bfloat16
LINK = jnp.int16
TOP = 32767.0
TINY = 1e-33
AHEAD = 2
EARLY = 2
LAG = 4


def kernel(
    rows_of, cols_of, owner_ref, list_ref, count_ref, mask_ref, amp, panel, out,
    both, maskv, ahead, mask_ahead, meta, meta_in, piece_in, half_s, half_f, got_s, got_f, fac_a, fac_t, fac_l, fac_c,
    p_a, p_t, p_l, p_c, w_a, w_t, w_l, w_c, local, t_own, s_out, s_scale, r_one, r_one_scale, t_out, t_scale, r_two, r_two_scale, leg, leg_scale, result,
    amp_sem, amp_send, amp_recv, ahead_send, ahead_recv, pass_send, pass_recv,
    a2a_send, a2a_recv, shift_send, shift_recv, ring_send, ring_recv, one_send, one_recv, two_send, two_recv, leg_send, leg_recv, out_sem,
):
    r, c = lax.axis_index("row"), lax.axis_index("col")
    depth_z = rows_of // 2
    chips = cols_of // 2
    y, z = r // depth_z, r % depth_z
    chip, core = c // 2, c % 2
    y_lo = chip % 2
    tile = panel.shape[-1]
    strip = tile // depth_z
    blocks, tiles = mask_ref.shape
    block = amp.shape[0] // blocks
    width = amp.shape[1]

    def at_chip(step, same_core=True):
        return lax.rem(chip + step + chips, chips) * 2 + core

    lane = lax.broadcasted_iota(jnp.int32, (8, 128), 1)
    flags = jnp.zeros((8, 128), F32)
    for k in range(2):
        live = jnp.where(k < count_ref[0, 0], k * tiles + list_ref[0, 0, k], -1)
        flags = flags + jnp.where(lane == live, 1.0, 0.0)
    meta[...] = flags
    meta_in[z] = flags
    for t in range(tiles):
        maskv[core, :, t * tile : (t + 1) * tile] = jnp.broadcast_to(
            mask_ref[:, t : t + 1].astype(F32), (blocks, tile)
        )

    own_amp = pltpu.make_async_copy(amp, both.at[core], amp_sem.at[0])
    own_amp.start()
    own_piece = pltpu.make_async_copy(
        panel.at[:, pl.ds(pl.multiple_of(z * strip, strip), strip), :], piece_in.at[z], amp_sem.at[1]
    )
    own_piece.start()

    barrier = pltpu.get_barrier_semaphore()

    across = lax.rem(r + depth_z, rows_of)

    def z_peer(d):
        return lax.rem(z + d, depth_z)

    def greet(d, carry):
        pl.semaphore_signal(barrier, 1, device_id=(y * depth_z + z_peer(d), c), device_id_type=MESH)
        return carry

    lax.fori_loop(1, depth_z, greet, 0)
    for step in (1, -1, 2, -2):
        for row in (r, across):
            pl.semaphore_signal(barrier, 1, device_id=(row, at_chip(step)), device_id_type=MESH)
    partner = chip * 2 + 1 - core
    pl.semaphore_signal(barrier, 1, device_id=(across, c), device_id_type=MESH)
    pl.semaphore_signal(barrier, 1, device_id=(r, partner), device_id_type=MESH)
    pl.semaphore_wait(barrier, depth_z - 1 + 10)

    def piece_copies(d):
        peer = z_peer(d)
        return (
            pltpu.make_async_remote_copy(
                src_ref=panel.at[:, pl.ds(pl.multiple_of(peer * strip, strip), strip), :],
                dst_ref=piece_in.at[z],
                send_sem=a2a_send.at[0, d],
                recv_sem=a2a_recv.at[0, d],
                device_id=(y * depth_z + peer, c),
                device_id_type=MESH,
            ),
            pltpu.make_async_remote_copy(
                src_ref=meta.at[pl.ds(0, 1)],
                dst_ref=meta_in.at[z, pl.ds(0, 1)],
                send_sem=a2a_send.at[1, d],
                recv_sem=a2a_recv.at[1, d],
                device_id=(y * depth_z + peer, c),
                device_id_type=MESH,
            ),
        )

    def send_pieces(d, carry):
        for copy in piece_copies(d):
            copy.start()
        return carry

    lax.fori_loop(1, depth_z, send_pieces, 0)

    swaps = (
        pltpu.make_async_remote_copy(
            src_ref=maskv.at[core], dst_ref=maskv.at[core], send_sem=amp_send.at[0], recv_sem=amp_recv.at[0],
            device_id=(r, partner), device_id_type=MESH,
        ),
        pltpu.make_async_remote_copy(
            src_ref=amp, dst_ref=both.at[core], send_sem=amp_send.at[1], recv_sem=amp_recv.at[1],
            device_id=(r, partner), device_id_type=MESH,
        ),
    )
    for copy in swaps:
        copy.start()

    def rows(i):
        return pl.ds(pl.multiple_of(i * block, block), block)

    def half_rows(n):
        return pl.ds(pl.multiple_of(n * (block // 2), block // 2), block // 2)

    def ahead_copy(n):
        return pltpu.make_async_remote_copy(
            src_ref=amp.at[half_rows(n)], dst_ref=ahead.at[core, half_rows(n)], send_sem=ahead_send.at[n],
            recv_sem=ahead_recv.at[n], device_id=(r, at_chip(1)), device_id_type=MESH,
        )

    def pass_copy(n):
        return pltpu.make_async_remote_copy(
            src_ref=ahead.at[core, half_rows(n)], dst_ref=ahead.at[core, half_rows(n)], send_sem=pass_send.at[n],
            recv_sem=pass_recv.at[n], device_id=(r, partner), device_id_type=MESH,
        )

    mask_copy = pltpu.make_async_remote_copy(
        src_ref=maskv.at[core], dst_ref=mask_ahead.at[core], send_sem=ahead_send.at[2 * AHEAD], recv_sem=ahead_recv.at[2 * AHEAD],
        device_id=(r, at_chip(1)), device_id_type=MESH,
    )
    mask_pass = pltpu.make_async_remote_copy(
        src_ref=mask_ahead.at[core], dst_ref=mask_ahead.at[core], send_sem=pass_send.at[2 * AHEAD],
        recv_sem=pass_recv.at[2 * AHEAD], device_id=(r, partner), device_id_type=MESH,
    )
    mask_copy.start()
    for n in range(EARLY):
        ahead_copy(n).start()

    def wait_pieces(d, carry):
        for copy in piece_copies(d):
            copy.wait_recv()
        return carry

    own_piece.wait()
    lax.fori_loop(1, depth_z, wait_pieces, 0)

    def chosen(even_step, odd_step):
        holder = owner_ref[pl.ds(even_step * (1 - core) + odd_step * core, 1), :] - y * depth_z
        wide = jnp.broadcast_to(holder, (strip, tile))
        small = jnp.broadcast_to(holder, (1, 128))
        first, second, factors = jnp.zeros((strip, tile), BF16), jnp.zeros((strip, tile), BF16), jnp.zeros((1, 128), F32)
        for j in range(depth_z):
            named = jnp.where(wide == j, 1.0, 0.0).astype(BF16)
            first = first + named * piece_in[j, 0]
            second = second + named * piece_in[j, 1]
            factors = factors + jnp.where(small == j, meta_in[j, 0:1], 0.0)
        return first, second, factors

    for slot, steps in enumerate(((2, 3), (1, 2), (0, 1), (3, 0))):
        half_s[slot, 0], half_s[slot, 1], half_f[slot, 0:1] = chosen(*steps)

    def halves(first, count, landing, step, n):
        out = []
        for m, row in enumerate((r, across)):
            for k, (src, dst) in enumerate(((half_s, got_s), (half_f, got_f))):
                out.append(
                    pltpu.make_async_remote_copy(
                        src_ref=src.at[(pl.ds(first, count), pl.ds(0, 1))[: 1 + k]],
                        dst_ref=dst.at[(m, pl.ds(landing, count), pl.ds(0, 1))[: 2 + k]],
                        send_sem=shift_send.at[n, m, k], recv_sem=shift_recv.at[n, m, k],
                        device_id=(row, at_chip(step)), device_id_type=MESH,
                    )
                )
        return out

    back_one = (halves(0, 1, 0, -1, 0), halves(1, 1, 1, -1, 3))
    stay = halves(0, 3, 2, 0, 1)[2:]
    stay_odd = halves(3, 1, 5, 0, 2)[2:]
    back_two = halves(3, 1, 5, -2, 2)
    for copy in back_one[0] + back_one[1]:
        copy.start()

    @pl.when(core == 0)
    def _():
        for copy in back_two:
            copy.start()

    for copy in stay:
        copy.start()

    @pl.when(core == 1)
    def _():
        for copy in stay_odd:
            copy.start()

    turn = 1 - 2 * core
    if depth_z > 4:
        hops = [(0, 2), (0, -2), (0, 1), (0, -1), (2, 1), (-2, -1), (2 * turn, 2 * turn)]
    else:
        hops = [(0, 2 * turn), (0, 1), (0, -1)]
    direct = 4 if depth_z > 4 else 3

    def strips_of(which, back):
        buf, slot = ((p_a, 0), (p_a, 1), (p_t, 0), (p_l, 0), (p_c, 0), (p_c, 1))[which]
        return buf.at[lax.rem(z - back + depth_z, depth_z), slot]

    def hop_copy(which, n):
        behind, on = hops[n]
        held = strips_of(which, behind)
        return pltpu.make_async_remote_copy(
            src_ref=held, dst_ref=held, send_sem=ring_send.at[which, n], recv_sem=ring_recv.at[which, n],
            device_id=(y * depth_z + lax.rem(z + on + depth_z, depth_z), c), device_id_type=MESH,
        )

    def hop_received(which, n):
        behind, on = hops[n]
        held = strips_of(which, behind + on)
        pltpu.make_async_remote_copy(
            src_ref=held, dst_ref=held, send_sem=ring_send.at[which, n], recv_sem=ring_recv.at[which, n],
            device_id=(r, partner), device_id_type=MESH,
        ).wait_recv()

    def ring_first(which):
        for n in range(direct):
            hop_copy(which, n).start()

    def ring_second(which):
        if direct < len(hops):
            hop_received(which, 0)
            hop_received(which, 1)
        for n in range(direct, len(hops)):
            hop_copy(which, n).start()

    def ring_rest(which):
        for n in range(len(hops)):
            if direct == len(hops) or n not in (0, 1):
                hop_received(which, n)

    def ring_drain(which):
        for n in range(len(hops)):
            hop_copy(which, n).wait_send()

    def assemble(fac, strips, weights, *slots):
        for slot in slots:
            factors = []
            for k in range(2):
                for t in range(tiles):
                    f = fac[slot, 0:1, k * tiles + t : k * tiles + t + 1]
                    factors.append(jnp.broadcast_to(f, (strip, tile)).astype(BF16))

            def put(i, carry):
                first, second = strips[i, slot, 0], strips[i, slot, 1]
                for t in range(tiles):
                    weights[slot, pl.ds(pl.multiple_of(t * tile + i * strip, strip), strip), :] = (
                        first * factors[t] + second * factors[tiles + t]
                    )
                return carry

            lax.fori_loop(0, depth_z, put, 0)

    def masked(group, i, mask=maskv, held=both):
        m = jnp.broadcast_to(mask[group, pl.ds(i, 1), :], (16, width)).astype(BF16)
        a = held[group, rows(i), :]
        return (a.reshape(block // 16, 16, width) * m[None]).reshape(block, width)

    def coded(x):
        peak = jnp.maximum(jnp.max(jnp.abs(x), axis=0, keepdims=True), TINY)
        return jnp.round(x * (TOP / peak)).astype(jnp.int32).astype(LINK), peak * (1.0 / TOP)

    one_chip = 1 - 2 * y_lo * (1 - core)

    def by_x(i):
        return (core == 1) & (y_lo == 1) & (lax.rem(i, 2) == 1)

    def first_leg(i):
        return [
            pltpu.make_async_remote_copy(
                src_ref=src, dst_ref=dst, send_sem=leg_send.at[k, i], recv_sem=leg_recv.at[k, i],
                device_id=(r, at_chip(2)), device_id_type=MESH,
            )
            for k, (src, dst) in enumerate(
                ((s_out.at[rows(i)], leg.at[rows(i)]), (s_scale.at[i, pl.ds(0, 1)], leg_scale.at[i, pl.ds(0, 1)]))
            )
        ]

    def second_leg(i):
        return [
            pltpu.make_async_remote_copy(
                src_ref=src, dst_ref=dst, send_sem=one_send.at[k, i], recv_sem=one_recv.at[k, i],
                device_id=(r, at_chip(-1)), device_id_type=MESH,
            )
            for k, (src, dst) in enumerate(
                ((leg.at[rows(i)], r_one.at[rows(i)]), (leg_scale.at[i, pl.ds(0, 1)], r_one_scale.at[i, pl.ds(0, 1)]))
            )
        ]

    def pass_on(i):
        @pl.when(by_x(i))
        def _():
            for first, second in zip(first_leg(i), second_leg(i)):
                first.wait_recv()
                second.start()

    def flow_one(i):
        where = (r, at_chip(one_chip))
        return (
            pltpu.make_async_remote_copy(
                src_ref=s_out.at[rows(i)], dst_ref=r_one.at[rows(i)], send_sem=one_send.at[0, i],
                recv_sem=one_recv.at[0, i], device_id=where, device_id_type=MESH,
            ),
            pltpu.make_async_remote_copy(
                src_ref=s_scale.at[i, pl.ds(0, 1)], dst_ref=r_one_scale.at[i, pl.ds(0, 1)], send_sem=one_send.at[1, i],
                recv_sem=one_recv.at[1, i], device_id=where, device_id_type=MESH,
            ),
        )

    def flow_two(i):
        where = (r, at_chip(2))
        return (
            pltpu.make_async_remote_copy(
                src_ref=t_out.at[rows(i)], dst_ref=r_two.at[rows(i)], send_sem=two_send.at[0, i],
                recv_sem=two_recv.at[0, i], device_id=where, device_id_type=MESH,
            ),
            pltpu.make_async_remote_copy(
                src_ref=t_scale.at[i, pl.ds(0, 1)], dst_ref=r_two_scale.at[i, pl.ds(0, 1)], send_sem=two_send.at[1, i],
                recv_sem=two_recv.at[1, i], device_id=where, device_id_type=MESH,
            ),
        )

    for slot in (0, 1):
        for copy in back_one[slot]:
            copy.wait_recv()
        p_a[z, slot] = got_s[0, slot] + got_s[1, slot]
        fac_a[slot, 0:1] = got_f[0, slot, 0:1] + got_f[1, slot, 0:1]
        ring_first(slot)
    ring_second(0)

    @pl.when(core == 0)
    def _():
        for copy in back_two:
            copy.wait_recv()
        p_t[z, 0] = got_s[0, 5] + got_s[1, 5]
        fac_t[0, 0:1] = got_f[0, 5, 0:1] + got_f[1, 5, 0:1]

    @pl.when(core == 1)
    def _():
        for copy in stay_odd:
            copy.wait_recv()
        p_t[z, 0] = half_s[3] + got_s[1, 5]
        fac_t[0, 0:1] = half_f[3, 0:1] + got_f[1, 5, 0:1]

    for copy in stay:
        copy.wait_recv()
    for n in range(EARLY, 2 * AHEAD):
        ahead_copy(n).start()
    p_l[z, 0] = half_s[2] + got_s[1, 4]
    fac_l[0, 0:1] = half_f[2, 0:1] + got_f[1, 4, 0:1]
    for slot in (0, 1):
        p_c[z, slot] = half_s[slot] + got_s[1, 2 + slot]
        fac_c[slot, 0:1] = half_f[slot, 0:1] + got_f[1, 2 + slot, 0:1]
    ring_second(1)
    ring_rest(0)
    assemble(fac_a, p_a, w_a, 0)
    ring_first(2)
    ring_rest(1)
    assemble(fac_a, p_a, w_a, 1)
    own_amp.wait()
    for copy in swaps:
        copy.wait_recv()

    def outward(i):
        x = jnp.dot(masked(0, i), w_a[0], preferred_element_type=F32)
        x = x + jnp.dot(masked(1, i), w_a[1], preferred_element_type=F32)
        code, scale = coded(x)
        s_out[rows(i)] = code
        s_scale[i, 0:1] = scale
        @pl.when(by_x(i))
        def _():
            for copy in first_leg(i):
                copy.start()

        @pl.when(jnp.logical_not(by_x(i)))
        def _():
            for copy in flow_one(i):
                copy.start()

    def received(buf, scale, i):
        return buf[rows(i)].astype(jnp.int32).astype(F32) * scale[i, 0:1]

    def send_two(i, x):
        code, scale = coded(x)
        t_out[rows(i)] = code
        t_scale[i, 0:1] = scale
        for copy in flow_two(i):
            copy.start()

    def odd_term(i, direct):
        x = jnp.dot(masked(1, i), w_t[0], preferred_element_type=F32)
        t_own[rows(i)] = x

        @pl.when((core == 0) if direct else ((core == 0) & (y_lo == 1)))
        def _():
            send_two(i, x)

    def relay(i):
        @pl.when((core == 0) & (y_lo == 0))
        def _():
            for copy in flow_one(i):
                copy.wait_recv()
            send_two(i, t_own[rows(i)] + received(r_one, r_one_scale, i))

    def result_copy(i):
        return pltpu.make_async_copy(result.at[rows(i)], out.at[rows(i)], out_sem.at[i])

    def here(i):
        x = jnp.dot(masked(0, i), w_l[0], preferred_element_type=F32)

        @pl.when(core == 1)
        def _():
            local[rows(i)] = x + t_own[rows(i)]

        @pl.when(core == 0)
        def _():
            local[rows(i)] = x

    def finish(i, early):
        if not early:

            @pl.when(y_lo + core > 0)
            def _():
                for copy in flow_one(i):
                    copy.wait_recv()
                local[rows(i)] = local[rows(i)] + received(r_one, r_one_scale, i)

        @pl.when(core == 0)
        def _():
            for copy in flow_two(i):
                copy.wait_recv()
            local[rows(i)] = local[rows(i)] + received(r_two, r_two_scale, i)

        result[rows(i)] = local[rows(i)].astype(BF16)
        result_copy(i).start()

    def each(first, last, *calls):
        def body(i, carry):
            for call in calls:
                call(i)
            return carry

        lax.fori_loop(first, last, body, 0)

    late = blocks - AHEAD
    cuts = [AHEAD + late * k // 4 for k in range(5)]
    @pl.when(core == 0)
    def _():
        each(cuts[0], cuts[1], outward)

    ring_second(2)
    for which in (3, 4, 5):
        ring_first(which)
    @pl.when(core == 0)
    def _():
        each(cuts[1], cuts[2], outward)

    @pl.when(core == 1)
    def _():
        each(cuts[0], cuts[2], outward)

    ring_rest(2)
    assemble(fac_t, p_t, w_t, 0)
    each(0, AHEAD, lambda i: odd_term(i, True))
    each(cuts[0], cuts[1], lambda i: odd_term(i, False))
    each(cuts[0], cuts[1], pass_on)
    each(cuts[2], cuts[3], outward)
    for which in (3, 4, 5):
        ring_second(which)
    each(cuts[1], cuts[2], lambda i: odd_term(i, False))
    each(cuts[3], cuts[4], outward)
    each(cuts[1], cuts[2], pass_on)
    mask_copy.wait_recv()
    mask_pass.start()
    for n in range(2 * AHEAD):
        ahead_copy(n).wait_recv()
        pass_copy(n).start()
    each(cuts[2], cuts[4], lambda i: odd_term(i, False))
    each(cuts[0], cuts[1], relay)
    ring_rest(3)
    assemble(fac_l, p_l, w_l, 0)
    each(0, blocks, here)
    each(cuts[1], cuts[2], relay)
    ring_rest(4)
    ring_rest(5)
    assemble(fac_c, p_c, w_c, 0, 1)
    mask_pass.wait_recv()

    def from_ahead(i):
        pass_copy(2 * i).wait_recv()
        pass_copy(2 * i + 1).wait_recv()
        local[rows(i)] = (
            local[rows(i)]
            + jnp.dot(masked(0, i, mask_ahead, ahead), w_c[0], preferred_element_type=F32)
            + jnp.dot(masked(1, i, mask_ahead, ahead), w_c[1], preferred_element_type=F32)
        )
        finish(i, True)

    each(cuts[2], cuts[3], pass_on)
    each(0, AHEAD, from_ahead)
    ready = cuts[2] - LAG
    assert ready >= AHEAD
    each(AHEAD, ready, lambda i: finish(i, False))
    each(cuts[3], cuts[4], pass_on)
    each(cuts[2], blocks, relay, lambda i: finish(i - LAG, False))
    each(blocks - LAG, blocks, lambda i: finish(i, False))

    def drain_pieces(d, carry):
        for copy in piece_copies(d):
            copy.wait_send()
        return carry

    lax.fori_loop(1, depth_z, drain_pieces, 0)
    for copy in list(swaps) + back_one[0] + back_one[1] + stay:
        copy.wait_send()

    @pl.when(core == 0)
    def _():
        for copy in back_two:
            copy.wait_send()

    @pl.when(core == 1)
    def _():
        for copy in stay_odd:
            copy.wait_send()

    for which in range(6):
        ring_drain(which)
    for copy in (mask_copy, mask_pass):
        copy.wait_send()
    for n in range(2 * AHEAD):
        ahead_copy(n).wait_send()
        pass_copy(n).wait_send()

    def drain_one(i, carry):
        @pl.when(by_x(i))
        def _():
            for copy in first_leg(i):
                copy.wait_send()

        for copy in flow_one(i):
            copy.wait_send()
        return carry

    lax.fori_loop(AHEAD, blocks, drain_one, 0)

    def drain_two(i, carry):
        @pl.when(core == 0)
        def _():
            for copy in flow_two(i):
                copy.wait_send()

        result_copy(i).wait()
        return carry

    lax.fori_loop(0, blocks, drain_two, 0)


def shards(rows_of, cols_of, amplitudes, pair_mask, integrals, tile_list, tile_count, owner):
    count, width = amplitudes.shape
    tile = integrals.shape[-1]
    blocks, tiles = pair_mask.shape
    block = count // blocks
    depth_z = rows_of // 2
    strip = tile // depth_z
    hops = 7 if depth_z > 4 else 3
    dma = pltpu.SemaphoreType.DMA
    vmem = pltpu.VMEM
    near = pl.BlockSpec(memory_space=pltpu.VMEM)
    smem = pl.BlockSpec(memory_space=pltpu.SMEM)
    away = pl.BlockSpec(memory_space=pl.ANY)
    code = vmem((count, tile), LINK)
    scale = vmem((blocks, 8, tile), F32)

    def strips(slots):
        return vmem((depth_z, slots, 2, strip, tile), BF16)

    return pl.pallas_call(
        functools.partial(kernel, rows_of, cols_of),
        out_shape=jax.ShapeDtypeStruct((count, tile), BF16),
        in_specs=[near, smem, smem, near, away, away],
        out_specs=away,
        scratch_shapes=[
            vmem((2, count, width), BF16),
            vmem((2, blocks, width), F32),
            vmem((2, AHEAD * block, width), BF16),
            vmem((2, blocks, width), F32),
            vmem((8, 128), F32),
            vmem((depth_z, 8, 128), F32),
            vmem((depth_z, 2, strip, tile), BF16),
            vmem((4, 2, strip, tile), BF16),
            vmem((4, 8, 128), F32),
            vmem((2, 6, 2, strip, tile), BF16),
            vmem((2, 6, 8, 128), F32),
            vmem((2, 8, 128), F32),
            vmem((1, 8, 128), F32),
            vmem((1, 8, 128), F32),
            vmem((2, 8, 128), F32),
            strips(2), strips(1), strips(1), strips(2),
            vmem((2, width, tile), BF16),
            vmem((1, width, tile), BF16),
            vmem((1, width, tile), BF16),
            vmem((2, width, tile), BF16),
            vmem((count, tile), F32),
            vmem((count, tile), F32),
            code, scale, code, scale, code, scale, code, scale, code, scale,
            vmem((count, tile), BF16),
            dma((2,)), dma((2,)), dma((2,)),
            dma((2 * AHEAD + 1,)), dma((2 * AHEAD + 1,)), dma((2 * AHEAD + 1,)), dma((2 * AHEAD + 1,)),
            dma((2, depth_z)), dma((2, depth_z)),
            dma((4, 2, 2)), dma((4, 2, 2)),
            dma((6, hops)), dma((6, hops)),
            dma((2, blocks)), dma((2, blocks)),
            dma((2, blocks)), dma((2, blocks)),
            dma((2, blocks)), dma((2, blocks)),
            dma((blocks,)),
        ],
        compiler_params=pltpu.CompilerParams(
            collective_id=0, has_side_effects=True, vmem_limit_bytes=56 * 1024 * 1024
        ),
    )(owner, tile_list, tile_count, pair_mask, amplitudes, integrals.reshape(integrals.shape[2:]))


def solution(mesh):
    return jax.shard_map(
        functools.partial(shards, mesh.shape["row"], mesh.shape["col"]),
        mesh=mesh,
        in_specs=(
            P("row", "col"),
            P("row", "col"),
            P("row", "col", None, None, None),
            P("row", "col", None),
            P("row", "col"),
            P(None, "col"),
        ),
        out_specs=P("row", "col"),
        check_vma=False,
    )
```
